32 devices in a mesh: gx: 2 (over core), gy: 16 (over z, y, x).
Axes of the slice: x: 2, y: 2, z: 4, core: 2. Of those that a mesh axis runs over, the one named last changes fastest.
Arguments:
- state: float32 [8, 2, 256, 256], P(None, None, 'gy', 'gx'), as said below
- offsets: int32 [2], replicated, may hold values from 0 to 255
Outputs:
- updated: float32 [8, 2, 256, 256], P(None, None, 'gy', 'gx')
The draws below stay inside these ranges and needn't reach their ends.
Inputs may be any that keep to these rules, and one draw needn't show every extreme that they name: `state`: density lies in [0.5, 2]; each momentum over density differs from the background (0 for x and z, -1.5 x_i for y with x_i = (i + 0.5)/256 - 0.5) by at most 0.3; face fields lie in [-0.5, 0.5]; energy exceeds kinetic plus cell-centred magnetic energy by a pressure of 0.5 to 1.5 over (5/3 - 1).
All inputs are finite; a program needn't handle non-finite values.
Results may differ from the reference program's by a relative error of at most 0.00002.
Values sent between devices are 32-bit elements; how exact they have to be, the bound alone decides.
A program may use at most 64 MiB of HBM per device.

```python
import jax
import jax.numpy as jnp
from jax import lax

CZ = 2
NX = 256
NY = 256
N_GY = 16


ADIABATIC = 5.0 / 3.0


def draw_state(key, part):
    streams = jax.random.split(key, 5)
    extent = (CZ, NY, NX)
    density = jax.random.uniform(streams[0], extent, dtype=jnp.float32, minval=0.5, maxval=2.0)
    magnetic = jax.random.uniform(streams[2], (3,) + extent, dtype=jnp.float32, minval=-0.5, maxval=0.5)
    pressure = jax.random.uniform(streams[3], extent, dtype=jnp.float32, minval=0.5, maxval=1.5)
    velocity = jax.random.uniform(streams[1], (3,) + extent, dtype=jnp.float32, minval=-0.3, maxval=0.3)
    position = (jnp.arange(NX, dtype=jnp.float32) + 0.5) / NX - 0.5
    velocity = velocity.at[1].add(-1.5 * position)
    centre_x = 0.5 * (magnetic[0] + jnp.roll(magnetic[0], -1, axis=2))
    centre_y = 0.5 * (magnetic[1] + jnp.roll(magnetic[1], -1, axis=1))
    centre_z = 0.5 * (magnetic[2] + jnp.roll(magnetic[2], -1, axis=0))
    magnetic_sq = centre_x * centre_x + centre_y * centre_y + centre_z * centre_z
    energy = pressure / (ADIABATIC - 1.0) + 0.5 * density * jnp.sum(velocity * velocity, axis=0) + 0.5 * magnetic_sq
    return jnp.concatenate([density[None], density * velocity, energy[None], magnetic], axis=0).astype(jnp.float32)


def setup_inputs(seed: int = 0) -> dict:
    streams_of = jax.random.split(jax.random.key(seed), 3)
    return {
        "state": draw_state(jax.random.fold_in(streams_of[2], 71), 0),
        "offsets": jax.random.randint(streams_of[1], (2,), 0, NY).astype(jnp.int32),
    }


ADIABATIC = 5.0 / 3.0
SIGNAL_SPEED = 4.0
COURANT_RATIO = 0.06
SHEAR_SPEED = 1.5


def physical_flux(conserved, direction):
    density = conserved[0]
    momenta = conserved[1:4]
    energy = conserved[4]
    magnetic = conserved[5:8]
    velocity = momenta / density
    magnetic_sq = jnp.sum(magnetic * magnetic, axis=0)
    pressure = (ADIABATIC - 1.0) * (energy - 0.5 * jnp.sum(momenta * velocity, axis=0) - 0.5 * magnetic_sq)
    total_pressure = pressure + 0.5 * magnetic_sq
    normal_speed = velocity[direction]
    normal_field = magnetic[direction]
    selector = (jnp.arange(3) == direction).astype(conserved.dtype)[:, None, None, None]
    momentum_flux = momenta * normal_speed - magnetic * normal_field + selector * total_pressure
    energy_flux = (energy + total_pressure) * normal_speed - normal_field * jnp.sum(velocity * magnetic, axis=0)
    induction = normal_speed * magnetic - velocity * normal_field
    return jnp.concatenate([momenta[direction][None], momentum_flux, energy_flux[None], induction], axis=0)


def advance(padded):
    centre_x = 0.5 * (padded[5, :, 1:-1, 1:-1] + padded[5, :, 1:-1, 2:])
    centre_y = 0.5 * (padded[6, :, 1:-1, 1:-1] + padded[6, :, 2:, 1:-1])
    centre_z = 0.5 * (padded[7, :, 1:-1, 1:-1] + jnp.roll(padded[7], -1, axis=0)[:, 1:-1, 1:-1])
    conserved = jnp.concatenate([padded[0:5, :, 1:-1, 1:-1], jnp.stack([centre_x, centre_y, centre_z])], axis=0)
    flux_phys = physical_flux(conserved, 0)
    face_x = 0.5 * (flux_phys[..., :-1] + flux_phys[..., 1:]) - 0.5 * SIGNAL_SPEED * (conserved[..., 1:] - conserved[..., :-1])
    flux_phys = physical_flux(conserved, 1)
    face_y = 0.5 * (flux_phys[:, :, :-1] + flux_phys[:, :, 1:]) - 0.5 * SIGNAL_SPEED * (conserved[:, :, 1:] - conserved[:, :, :-1])
    flux_phys = physical_flux(conserved, 2)
    face_z = 0.5 * (jnp.roll(flux_phys, 1, axis=1) + flux_phys) - 0.5 * SIGNAL_SPEED * (conserved - jnp.roll(conserved, 1, axis=1))
    divergence = (face_x[:5, :, 1:-1, 1:] - face_x[:5, :, 1:-1, :-1]) + (face_y[:5, :, 1:, 1:-1] - face_y[:5, :, :-1, 1:-1])
    divergence = divergence + (jnp.roll(face_z[:5], -1, axis=1) - face_z[:5])[:, :, 1:-1, 1:-1]
    hydro = padded[0:5, :, 2:-2, 2:-2] - COURANT_RATIO * divergence
    emf_z = 0.25 * (-(face_x[6, :, 1:, :] + face_x[6, :, :-1, :]) + (face_y[5, :, :, 1:] + face_y[5, :, :, :-1]))
    emf_x = 0.25 * (-(face_y[7] + jnp.roll(face_y[7], 1, axis=0)) + (face_z[6, :, 1:, :] + face_z[6, :, :-1, :]))
    emf_y = 0.25 * ((face_x[7] + jnp.roll(face_x[7], 1, axis=0)) - (face_z[5, :, :, 1:] + face_z[5, :, :, :-1]))
    new_bx = padded[5, :, 2:-2, 2:-2] - COURANT_RATIO * ((emf_z[:, 1:, :-1] - emf_z[:, :-1, :-1]) - (jnp.roll(emf_y, -1, axis=0) - emf_y)[:, 1:-1, :-1])
    new_by = padded[6, :, 2:-2, 2:-2] - COURANT_RATIO * ((jnp.roll(emf_x, -1, axis=0) - emf_x)[:, :-1, 1:-1] - (emf_z[:, :-1, 1:] - emf_z[:, :-1, :-1]))
    new_bz = padded[7, :, 2:-2, 2:-2] - COURANT_RATIO * ((emf_y[:, 1:-1, 1:] - emf_y[:, 1:-1, :-1]) - (emf_x[:, 1:, 1:-1] - emf_x[:, :-1, 1:-1]))
    return jnp.concatenate([hydro, jnp.stack([new_bx, new_by, new_bz])], axis=0)


def shear_correct(strip, sign):
    density = strip[0]
    along = strip[2]
    new_along = along + sign * SHEAR_SPEED * density
    new_energy = strip[4] + sign * SHEAR_SPEED * along + 0.5 * SHEAR_SPEED * SHEAR_SPEED * density
    return jnp.concatenate([strip[0:2], new_along[None], strip[3:4], new_energy[None], strip[5:8]], axis=0)


def section_update(field, shift):
    rows_all = field.shape[2]
    lower_ghost = shear_correct(jnp.roll(field[..., -2:], -shift, axis=2), 1.0)
    upper_ghost = shear_correct(jnp.roll(field[..., :2], shift, axis=2), -1.0)
    widened = jnp.concatenate([lower_ghost, field, upper_ghost], axis=3)
    wrapped = jnp.concatenate([widened[:, :, -2:], widened, widened[:, :, :2]], axis=2)
    rows_block = rows_all // N_GY

    def one_block(block_index):
        window = lax.dynamic_slice_in_dim(wrapped, block_index * rows_block, rows_block + 4, axis=2)
        return advance(window)

    blocks = lax.map(one_block, jnp.arange(N_GY, dtype=jnp.int32))
    return jnp.moveaxis(blocks, 0, 2).reshape(field.shape)


def reference(state, offsets):
    middle = section_update(state, offsets[0])
    final = section_update(middle, offsets[1])
    return 0.5 * (state + final)
```

```python
import functools

import jax
import jax.numpy as jnp
from jax import lax
from jax.experimental import pallas as pl
from jax.experimental.pallas import tpu as pltpu
from jax.sharding import PartitionSpec as P

ADIABATIC = 5.0 / 3.0
SIGNAL_SPEED = 4.0
COURANT_RATIO = 0.06
SHEAR_SPEED = 1.5
MESH = pl.DeviceIdType.MESH


def turned(value, shift, axis):
    return pltpu.roll(value, shift % value.shape[axis], axis)


def advance(fields, depth):
    xm = lambda a: turned(a, 1, 1)
    xp = lambda a: turned(a, -1, 1)
    ym = lambda a: turned(a, 1, 0)
    yp = lambda a: turned(a, -1, 0)
    half_a = 0.5 * SIGNAL_SPEED
    levels = range(depth)
    below = lambda z: (z - 1) % depth
    above = lambda z: (z + 1) % depth

    cells, flux_z, emf = [], [], []
    for z in levels:
        rho, mx, my, mz, en, bx, by, bz = (fields[f][z] for f in range(8))
        cx = 0.5 * (bx + xp(bx))
        cy = 0.5 * (by + yp(by))
        cz = 0.5 * (bz + fields[7][above(z)])
        inv = 1.0 / rho
        vx, vy, vz = mx * inv, my * inv, mz * inv
        bsq = cx * cx + cy * cy + cz * cz
        pressure = (ADIABATIC - 1.0) * (en - 0.5 * (mx * vx + my * vy + mz * vz) - 0.5 * bsq)
        pt = pressure + 0.5 * bsq
        vb = vx * cx + vy * cy + vz * cz
        ept = en + pt
        mxy = mx * vy - cx * cy
        mxz = mx * vz - cx * cz
        myz = my * vz - cy * cz
        flux_x = (mx, mx * vx - cx * cx + pt, mxy, mxz, ept * vx - cx * vb)
        flux_y = (my, mxy, my * vy - cy * cy + pt, myz, ept * vy - cy * vb)
        flux_v = (mz, mxz, myz, mz * vz - cz * cz + pt, ept * vz - cz * vb)
        q = (rho, mx, my, mz, en)
        total = []
        ups, downs = [], []
        for f in range(5):
            aq = half_a * q[f]
            hx, hy, hz = 0.5 * flux_x[f], 0.5 * flux_y[f], 0.5 * flux_v[f]
            face_x = xm(hx + aq) + (hx - aq)
            face_y = ym(hy + aq) + (hy - aq)
            total.append((xp(face_x) - face_x) + (yp(face_y) - face_y))
            ups.append(hz + aq)
            downs.append(hz - aq)
        gz = 0.5 * (vx * cy - vy * cx)
        gx = 0.5 * (vy * cz - vz * cy)
        gy = 0.5 * (vx * cz - vz * cx)
        ax, ay, az = half_a * cx, half_a * cy, half_a * cz
        fx_by = xm(gz + ay) + (gz - ay)
        fy_bx = ym(ax - gz) - (gz + ax)
        ez = 0.25 * ((fy_bx + xm(fy_bx)) - (fx_by + ym(fx_by)))
        fy_bz = ym(gx + az) + (gx - az)
        fx_bz = xm(gy + az) + (gy - az)
        cells.append((q, total, ups, downs))
        emf.append((ez, fy_bz, fx_bz, ay - gx, gx + ay, ax - gy, gy + ax))

    ex, ey = [], []
    for z in levels:
        fz_by = emf[below(z)][3] - emf[z][4]
        fz_bx = emf[below(z)][5] - emf[z][6]
        ex.append(0.25 * ((fz_by + ym(fz_by)) - (emf[z][1] + emf[below(z)][1])))
        ey.append(0.25 * ((emf[z][2] + emf[below(z)][2]) - (fz_bx + xm(fz_bx))))

    face_z = [
        [cells[below(z)][2][f] + cells[z][3][f] for f in range(5)] for z in levels
    ]
    out = [[None] * depth for _ in range(8)]
    for z in levels:
        q, total, _, _ = cells[z]
        for f in range(5):
            change = total[f] + (face_z[above(z)][f] - face_z[z][f])
            out[f][z] = q[f] - COURANT_RATIO * change
        ez = emf[z][0]
        dz_ey = ey[above(z)] - ey[z]
        dz_ex = ex[above(z)] - ex[z]
        out[5][z] = fields[5][z] - COURANT_RATIO * ((yp(ez) - ez) - dz_ey)
        out[6][z] = fields[6][z] - COURANT_RATIO * (dz_ex - (xp(ez) - ez))
        out[7][z] = fields[7][z] - COURANT_RATIO * ((xp(ey[z]) - ey[z]) - (yp(ex[z]) - ex[z]))
    return out


def kernel(
    nx, ny, offsets_ref, state_ref, out_ref, pack, rim_low, rim_high, own, left, right,
    send_own, recv_own, send_left, recv_left, send_right, recv_right, send_rim, recv_rim,
):
    depth, rows, lanes = state_ref.shape[1:]
    two = nx == 2
    cx, cy = lax.axis_index("gx"), lax.axis_index("gy")
    lx, rx = lax.rem(cx + nx - 1, nx), lax.rem(cx + 1, nx)
    up, down = lax.rem(cy + 1, ny), lax.rem(cy + ny - 1, ny)
    others = [rx] if two else [lx, rx]

    barrier = pltpu.get_barrier_semaphore()

    def greet(d, _):
        there = lax.rem(cy + d, ny)

        @pl.when(d > 0)
        def _():
            pl.semaphore_signal(barrier, inc=1, device_id=(cx, there), device_id_type=MESH)

        for column in others:
            pl.semaphore_signal(barrier, inc=1, device_id=(column, there), device_id_type=MESH)
        return 0

    lax.fori_loop(0, ny, greet, 0)

    lane = lax.broadcasted_iota(jnp.int32, (8, lanes), 1)
    sub = lane % 8
    part = lane // 8
    sublane = lax.broadcasted_iota(jnp.int32, (8, lanes), 0)
    mine = pl.multiple_of(cy * rows, rows)
    for t in range(0, rows, 8):
        packed = jnp.zeros((8, lanes), jnp.float32)
        for f in range(8):
            for z in range(depth):
                k = f * depth + z
                moved = turned(state_ref[f, z, t : t + 8, :], 8 * k + 4, 1)
                packed = jnp.where(part == k, moved, packed)
        pack[t : t + 8, :] = packed
        own[pl.ds(pl.multiple_of(mine + t, 8), 8), :] = packed

    pl.semaphore_wait(barrier, ny * (1 + len(others)) - 1)

    rims = [
        pltpu.make_async_remote_copy(
            src_ref=state_ref.at[:, :, pl.ds(rows - 8, 8), :], dst_ref=rim_low,
            send_sem=send_rim.at[0], recv_sem=recv_rim.at[0],
            device_id=(cx, up), device_id_type=MESH,
        ),
        pltpu.make_async_remote_copy(
            src_ref=state_ref.at[:, :, pl.ds(0, 8), :], dst_ref=rim_high,
            send_sem=send_rim.at[1], recv_sem=recv_rim.at[1],
            device_id=(cx, down), device_id_type=MESH,
        ),
    ]

    lines = [(own, cx, send_own, recv_own)]
    if two:
        lines.append((left, rx, send_left, recv_left))
    else:
        lines.append((left, rx, send_left, recv_left))
        lines.append((right, lx, send_right, recv_right))

    def strip_copy(line, target, source):
        buffer, column, send, recv = line
        return pltpu.make_async_remote_copy(
            src_ref=pack,
            dst_ref=buffer.at[pl.ds(pl.multiple_of(source * rows, rows), rows), :],
            send_sem=send.at[target], recv_sem=recv.at[source],
            device_id=(column, target), device_id_type=MESH,
        )

    def each(action):
        def step(d, _):
            there = lax.rem(cy + d, ny)

            @pl.when(d > 0)
            def _():
                action(lines[0], there)

            for line in lines[1:]:
                action(line, there)
            return 0

        lax.fori_loop(0, ny, step, 0)

    each(lambda line, there: strip_copy(line, there, cy).start())
    for copy in rims:
        copy.start()

    each(lambda line, there: strip_copy(line, there, there).wait_recv())
    for copy in rims:
        copy.wait_recv()

    total_rows = rows * ny
    for buffer, *_ in lines:
        buffer[total_rows : total_rows + 8, :] = buffer[0:8, :]
    left_buf = left
    right_buf = left if two else right

    at_lower = cx == 0
    at_upper = cx == nx - 1
    lower_i = at_lower.astype(jnp.int32)
    upper_i = at_upper.astype(jnp.int32)
    lower_f = at_lower.astype(jnp.float32)
    upper_f = at_upper.astype(jnp.float32)
    first, second = offsets_ref[0], offsets_ref[1]
    base = cy * rows

    def slab(buffer, shift):
        def part_at(j):
            return buffer[pl.ds(lax.rem(base + shift + (j + 2 * total_rows), total_rows), 8), :]

        edge = jnp.where(sublane < 4, part_at(rows), part_at(-8))
        return [part_at(t) for t in range(0, rows, 8)] + [edge]

    field_of = part // depth
    def corrected(tiles, sign):
        along = jnp.where((field_of == 2) | (field_of == 4), sign * SHEAR_SPEED, 0.0)
        square = jnp.where(field_of == 4, sign * sign * (0.5 * SHEAR_SPEED * SHEAR_SPEED), 0.0)
        return [
            p + along * turned(p, 16 * depth, 1) + square * turned(p, 32 * depth, 1) for p in tiles
        ]

    ghost_l = corrected(slab(left_buf, lower_i * first), lower_f)
    ghost_r = corrected(slab(right_buf, -upper_i * first), -upper_f)
    side = lower_i - upper_i
    side_f = lower_f - upper_f
    far = slab(left_buf, side * second)
    if not two:
        far_r = slab(right_buf, side * second)
        far = [jnp.where(at_upper, b, a) for a, b in zip(far, far_r)]
    near = corrected(slab(own, side * (second - first)), -side_f)

    ghosts = [
        jnp.where(sub < 4, turned(b, -4, 1), turned(a, 4, 1)) for a, b in zip(ghost_l, ghost_r)
    ]
    from_far = (sub < 4) == at_lower
    joint = [jnp.where(from_far, a, b) for a, b in zip(far, near)]

    stack = lambda tiles: jnp.concatenate(tiles, axis=0)
    ghosts, joint = stack(ghosts), stack(joint)
    height = rows + 8
    wide = lax.broadcasted_iota(jnp.int32, (height, lanes), 1)
    main, strip = [], []
    for f in range(8):
        main.append([])
        strip.append([])
        for z in range(depth):
            k = f * depth + z
            edge = jnp.where(sublane < 4, rim_high[f, z], rim_low[f, z])
            m = jnp.concatenate([state_ref[f, z], edge], axis=0)
            s = jnp.where(wide < 40, turned(m, 8, 1), m)
            s = jnp.where(wide < 8, turned(ghosts, -8 * k, 1), s)
            s = jnp.where((wide >= 40) & (wide < 48), turned(joint, 40 - 8 * k, 1), s)
            main[f].append(m)
            strip[f].append(s)

    main = advance(main, depth)
    strip = advance(strip, depth)
    back = jnp.where(at_lower, lanes - 36, lanes - 44)
    takes = ((wide == 7) & at_lower) | ((wide < 2) & at_upper)
    for z in range(depth):
        moved = [pltpu.roll(strip[f][z], back, 1) for f in range(8)]
        rho, my = moved[0], moved[2]
        moved[2] = my + (side_f * SHEAR_SPEED) * rho
        moved[4] = moved[4] + (side_f * SHEAR_SPEED) * my + (0.5 * SHEAR_SPEED * SHEAR_SPEED) * rho
        for f in range(8):
            strip[f][z] = jnp.where(takes, moved[f], strip[f][z])
    main = advance(main, depth)
    strip = advance(strip, depth)

    inner = wide[:rows]
    for f in range(8):
        for z in range(depth):
            s = strip[f][z][:rows]
            new = jnp.where(inner < 4, turned(s, -8, 1), jnp.where(inner >= lanes - 8, s, main[f][z][:rows]))
            out_ref[f, z] = 0.5 * (state_ref[f, z] + new)

    each(lambda line, there: strip_copy(line, there, cy).wait_send())
    for copy in rims:
        copy.wait_send()


def on_device(nx, ny, state, offsets):
    fields, depth, rows, lanes = state.shape
    dma = pltpu.SemaphoreType.DMA
    gathered = pltpu.VMEM((rows * ny + 8, lanes), jnp.float32)
    spare = gathered if nx > 2 else pltpu.VMEM((8, lanes), jnp.float32)
    return pl.pallas_call(
        functools.partial(kernel, nx, ny),
        out_shape=jax.ShapeDtypeStruct(state.shape, state.dtype),
        in_specs=[
            pl.BlockSpec(memory_space=pltpu.SMEM),
            pl.BlockSpec(memory_space=pltpu.VMEM),
        ],
        out_specs=pl.BlockSpec(memory_space=pltpu.VMEM),
        scratch_shapes=[
            pltpu.VMEM((rows, lanes), jnp.float32),
            pltpu.VMEM((fields, depth, 8, lanes), jnp.float32),
            pltpu.VMEM((fields, depth, 8, lanes), jnp.float32),
            gathered, gathered, spare,
            dma((ny,)), dma((ny,)), dma((ny,)), dma((ny,)), dma((ny,)), dma((ny,)),
            dma((2,)), dma((2,)),
        ],
        compiler_params=pltpu.CompilerParams(collective_id=0, has_side_effects=True),
    )(offsets, state)


def solution(mesh):
    nx, ny = mesh.shape["gx"], mesh.shape["gy"]
    return jax.shard_map(
        functools.partial(on_device, nx, ny),
        mesh=mesh,
        in_specs=(P(None, None, "gy", "gx"), P()),
        out_specs=P(None, None, "gy", "gx"),
        check_vma=False,
    )
```

```python
import functools

import jax
import jax.numpy as jnp
from jax import lax
from jax.experimental import pallas as pl
from jax.experimental.pallas import tpu as pltpu
from jax.sharding import PartitionSpec as P

ADIABATIC = 5.0 / 3.0
SIGNAL_SPEED = 4.0
COURANT_RATIO = 0.06
SHEAR_SPEED = 1.5
MESH = pl.DeviceIdType.MESH


def turned(value, shift, axis):
    return pltpu.roll(value, shift % value.shape[axis], axis)


def advance(fields, depth):
    xm = lambda a: turned(a, 1, 1)
    xp = lambda a: turned(a, -1, 1)
    ym = lambda a: turned(a, 1, 0)
    yp = lambda a: turned(a, -1, 0)
    half_a = 0.5 * SIGNAL_SPEED
    levels = range(depth)
    below = lambda z: (z - 1) % depth
    above = lambda z: (z + 1) % depth

    cells, flux_z, emf = [], [], []
    for z in levels:
        rho, mx, my, mz, en, bx, by, bz = (fields[f][z] for f in range(8))
        cx = 0.5 * (bx + xp(bx))
        cy = 0.5 * (by + yp(by))
        cz = 0.5 * (bz + fields[7][above(z)])
        inv = 1.0 / rho
        vx, vy, vz = mx * inv, my * inv, mz * inv
        bsq = cx * cx + cy * cy + cz * cz
        pressure = (ADIABATIC - 1.0) * (en - 0.5 * (mx * vx + my * vy + mz * vz) - 0.5 * bsq)
        pt = pressure + 0.5 * bsq
        vb = vx * cx + vy * cy + vz * cz
        ept = en + pt
        mxy = mx * vy - cx * cy
        mxz = mx * vz - cx * cz
        myz = my * vz - cy * cz
        flux_x = (mx, mx * vx - cx * cx + pt, mxy, mxz, ept * vx - cx * vb)
        flux_y = (my, mxy, my * vy - cy * cy + pt, myz, ept * vy - cy * vb)
        flux_v = (mz, mxz, myz, mz * vz - cz * cz + pt, ept * vz - cz * vb)
        q = (rho, mx, my, mz, en)
        total = []
        ups, downs = [], []
        for f in range(5):
            aq = half_a * q[f]
            hx, hy, hz = 0.5 * flux_x[f], 0.5 * flux_y[f], 0.5 * flux_v[f]
            face_x = xm(hx + aq) + (hx - aq)
            face_y = ym(hy + aq) + (hy - aq)
            total.append((xp(face_x) - face_x) + (yp(face_y) - face_y))
            ups.append(hz + aq)
            downs.append(hz - aq)
        gz = 0.5 * (vx * cy - vy * cx)
        gx = 0.5 * (vy * cz - vz * cy)
        gy = 0.5 * (vx * cz - vz * cx)
        ax, ay, az = half_a * cx, half_a * cy, half_a * cz
        fx_by = xm(gz + ay) + (gz - ay)
        fy_bx = ym(ax - gz) - (gz + ax)
        ez = 0.25 * ((fy_bx + xm(fy_bx)) - (fx_by + ym(fx_by)))
        fy_bz = ym(gx + az) + (gx - az)
        fx_bz = xm(gy + az) + (gy - az)
        cells.append((q, total, ups, downs))
        emf.append((ez, fy_bz, fx_bz, ay - gx, gx + ay, ax - gy, gy + ax))

    ex, ey = [], []
    for z in levels:
        fz_by = emf[below(z)][3] - emf[z][4]
        fz_bx = emf[below(z)][5] - emf[z][6]
        ex.append(0.25 * ((fz_by + ym(fz_by)) - (emf[z][1] + emf[below(z)][1])))
        ey.append(0.25 * ((emf[z][2] + emf[below(z)][2]) - (fz_bx + xm(fz_bx))))

    face_z = [
        [cells[below(z)][2][f] + cells[z][3][f] for f in range(5)] for z in levels
    ]
    out = [[None] * depth for _ in range(8)]
    for z in levels:
        q, total, _, _ = cells[z]
        for f in range(5):
            change = total[f] + (face_z[above(z)][f] - face_z[z][f])
            out[f][z] = q[f] - COURANT_RATIO * change
        ez = emf[z][0]
        dz_ey = ey[above(z)] - ey[z]
        dz_ex = ex[above(z)] - ex[z]
        out[5][z] = fields[5][z] - COURANT_RATIO * ((yp(ez) - ez) - dz_ey)
        out[6][z] = fields[6][z] - COURANT_RATIO * (dz_ex - (xp(ez) - ez))
        out[7][z] = fields[7][z] - COURANT_RATIO * ((xp(ey[z]) - ey[z]) - (yp(ex[z]) - ex[z]))
    return out


def kernel(
    nx, ny, offsets_ref, input_ref, out_ref, state_ref, packs, rim_up, rim_down, rim_low, rim_high,
    gather_low, gather_high, halo_left, halo_right, joined,
    send_edge, recv_edge, send_side, recv_side, send_rim, recv_rim, load_sem,
):
    fields, depth, rows, lanes = state_ref.shape
    cx, cy = lax.axis_index("gx"), lax.axis_index("gy")
    up, down = lax.rem(cy + 1, ny), lax.rem(cy + ny - 1, ny)
    at_lower = cx == 0
    at_upper = cx == nx - 1
    at_edge = at_lower | at_upper
    lower_i = at_lower.astype(jnp.int32)
    upper_i = at_upper.astype(jnp.int32)
    lower_f = at_lower.astype(jnp.float32)
    upper_f = at_upper.astype(jnp.float32)
    opposite = jnp.where(at_lower, nx - 1, 0)
    near_rows = (down, cy, up)

    def around(action):
        def step(d, _):
            there = lax.rem(cy + d, ny)
            action(opposite, there)

            @pl.when(d < ny)
            def _():
                action(cx, there)

            return 0

        if ny > 16:
            lax.fori_loop(1, ny + 1, step, 0)
            return
        for d in range(1, ny + 1):
            there = lax.rem(cy + d, ny)
            action(opposite, there)
            if d < ny:
                action(cx, there)

    barrier = pltpu.get_barrier_semaphore()

    def greet(column, row):
        pl.semaphore_signal(barrier, inc=1, device_id=(column, row), device_id_type=MESH)

    load = pltpu.make_async_copy(input_ref, state_ref, load_sem)
    load.start()
    if nx == 2:
        around(greet)
        greetings = 2 * ny - 1
    else:

        @pl.when(at_edge)
        def _():
            around(greet)

        @pl.when(jnp.logical_not(at_edge))
        def _():
            greet(cx, up)
            greet(cx, down)

        @pl.when(jnp.logical_not(at_lower))
        def _():
            for row in near_rows:
                greet(cx - 1, row)

        @pl.when(jnp.logical_not(at_upper))
        def _():
            for row in near_rows:
                greet(cx + 1, row)

        greetings = jnp.where(at_edge, 2 * ny - 1 + 3, 2 + 6)

    lane = lax.broadcasted_iota(jnp.int32, (8, lanes), 1)
    sub = lane % 8
    part = lane // 8
    sublane = lax.broadcasted_iota(jnp.int32, (8, lanes), 0)
    swapped = lambda p: jnp.where(sub < 4, turned(p, -4, 1), turned(p, 4, 1))
    load.wait()
    tiles = []
    for t in (0, 8):
        packed = jnp.zeros((8, lanes), jnp.float32)
        for k in range(fields * depth):
            moved = turned(state_ref[k // depth, k % depth, t : t + 8, :], 8 * k + 4, 1)
            packed = jnp.where(part == k, moved, packed)
        tiles.append(packed)
    front = swapped(tiles[0])
    low = jnp.where(sub < 4, front, tiles[1])
    high = jnp.where(sub < 4, tiles[1], front)
    packs[0] = low
    packs[1] = high
    own_rows = pl.ds(pl.multiple_of(cy * 8, 8), 8)

    @pl.when(at_lower)
    def _():
        gather_low[own_rows, :] = low

    @pl.when(at_upper)
    def _():
        gather_high[own_rows, :] = high

    spots = []
    for k in range(fields * depth):
        f, z = k // depth, k % depth
        count = 3 if f == 6 else 2
        spots.append((spots[-1][0] + spots[-1][1] if spots else 0, count))
        rim_up[2 * k : 2 * k + 2, :] = state_ref[f, z, rows - 2 : rows, :]
        rim_down[spots[k][0] : spots[k][0] + count, :] = state_ref[f, z, 0:count, :]

    pl.semaphore_wait(barrier, greetings)

    def edge_copy(buffer, side, column, target, source):
        return pltpu.make_async_remote_copy(
            src_ref=packs.at[side],
            dst_ref=buffer.at[pl.ds(pl.multiple_of(source * 8, 8), 8), :],
            send_sem=send_edge.at[(column == cx).astype(jnp.int32), target],
            recv_sem=recv_edge.at[side, source],
            device_id=(column, target), device_id_type=MESH,
        )

    def side_copy(buffer, side, column, n):
        return pltpu.make_async_remote_copy(
            src_ref=packs.at[side], dst_ref=buffer.at[2 - n],
            send_sem=send_side.at[side, n], recv_sem=recv_side.at[side, 2 - n],
            device_id=(column, near_rows[n]), device_id_type=MESH,
        )

    def at_sides(method):
        @pl.when(at_lower)
        def _():
            around(lambda c, r: method(edge_copy(gather_low, 0, c, r, cy)))

        @pl.when(at_upper)
        def _():
            around(lambda c, r: method(edge_copy(gather_high, 1, c, r, cy)))

        @pl.when(jnp.logical_not(at_lower))
        def _():
            for n in range(3):
                method(side_copy(halo_right, 0, cx - 1, n))

        @pl.when(jnp.logical_not(at_upper))
        def _():
            for n in range(3):
                method(side_copy(halo_left, 1, cx + 1, n))

    def arrivals(wait):
        def from_edge(c, r):
            @pl.when(c == 0)
            def _():
                wait(edge_copy(gather_low, 0, c, r, r))

            @pl.when(c != 0)
            def _():
                wait(edge_copy(gather_high, 1, c, r, r))

        @pl.when(at_edge)
        def _():
            around(from_edge)

        @pl.when(jnp.logical_not(at_upper))
        def _():
            for n in range(3):
                wait(side_copy(halo_right, 0, cx + 1, 2 - n))

        @pl.when(jnp.logical_not(at_lower))
        def _():
            for n in range(3):
                wait(side_copy(halo_left, 1, cx - 1, 2 - n))

    rims = [
        pltpu.make_async_remote_copy(
            src_ref=rim_up, dst_ref=rim_low.at[pl.ds(8, 2 * fields * depth), :],
            send_sem=send_rim.at[0], recv_sem=recv_rim.at[0],
            device_id=(cx, up), device_id_type=MESH,
        ),
        pltpu.make_async_remote_copy(
            src_ref=rim_down, dst_ref=rim_high,
            send_sem=send_rim.at[1], recv_sem=recv_rim.at[1],
            device_id=(cx, down), device_id_type=MESH,
        ),
    ]
    at_sides(lambda copy: copy.start())
    for copy in rims:
        copy.start()
    arrivals(lambda copy: copy.wait_recv())
    for copy in rims:
        copy.wait_recv()

    def unfold(low, high):
        return jnp.where(sub < 4, low, high), swapped(jnp.where(sub < 4, high, low))

    total_rows = rows * ny

    def lay(block):
        a, b = unfold(gather_low[pl.ds(block * 8, 8), :], gather_high[pl.ds(block * 8, 8), :])
        joined[pl.ds(block * rows, 8), :] = a
        joined[pl.ds(block * rows + 8, 8), :] = b

    if ny > 16:
        lax.fori_loop(0, ny, lambda b, _: (lay(b), 0)[1], 0)
    else:
        for block in range(ny):
            lay(block)
    joined[total_rows : total_rows + 8, :] = joined[0:8, :]

    first, second = offsets_ref[0], offsets_ref[1]
    base = cy * rows

    def slab(shift):
        def part_at(j):
            return joined[pl.ds(lax.rem(base + shift + (j + 2 * total_rows), total_rows), 8), :]

        edge = jnp.where(sublane < 4, part_at(rows), part_at(-8))
        return [part_at(0), part_at(8), edge]

    field_of = part // depth

    def corrected(tiles, sign):
        along = jnp.where((field_of == 2) | (field_of == 4), sign * SHEAR_SPEED, 0.0)
        square = jnp.where(field_of == 4, 0.5 * SHEAR_SPEED * SHEAR_SPEED, 0.0)
        return [
            p + along * turned(p, 8 * 2 * depth, 1) + square * turned(p, 8 * 4 * depth, 1)
            for p in tiles
        ]

    side = lower_i - upper_i
    side_f = lower_f - upper_f
    sheared = corrected(slab(side * first), side_f)
    far = slab(side * second)
    near = corrected(slab(side * (second - first)), -side_f)
    beside = [unfold(halo_right[n], halo_left[n]) for n in range(3)]
    plain = [beside[1][0], beside[1][1], jnp.where(sublane < 4, beside[2][0], beside[0][1])]
    is_low = sub < 4
    from_shear = (is_low & at_upper) | (jnp.logical_not(is_low) & at_lower)
    ghosts = [jnp.where(from_shear, a, b) for a, b in zip(sheared, plain)]
    joint = [swapped(jnp.where(is_low == at_upper, a, b)) for a, b in zip(far, near)]

    stack = lambda tiles: jnp.concatenate(tiles, axis=0)
    ghosts, joint = stack(ghosts), stack(joint)
    height = rows + 8
    wide = lax.broadcasted_iota(jnp.int32, (height, lanes), 1)
    main, strip = [], []
    for f in range(8):
        main.append([])
        strip.append([])
        for z in range(depth):
            k = f * depth + z
            after, before = spots[k][0], 2 * k + 2
            edge = jnp.where(
                sublane < 4, rim_high[after : after + 8, :], rim_low[before : before + 8, :]
            )
            m = jnp.concatenate([state_ref[f, z], edge], axis=0)
            s = jnp.where(wide < 40, turned(m, 8, 1), m)
            s = jnp.where(wide < 8, turned(ghosts, -8 * k, 1), s)
            s = jnp.where((wide >= 40) & (wide < 48), turned(joint, 40 - 8 * k, 1), s)
            main[f].append(m)
            strip[f].append(s)

    main = advance(main, depth)
    strip = advance(strip, depth)
    back = jnp.where(at_lower, lanes - 36, lanes - 44)
    takes = ((wide == 7) & at_lower) | ((wide < 2) & at_upper)
    for z in range(depth):
        moved = [pltpu.roll(strip[f][z], back, 1) for f in range(8)]
        rho, my = moved[0], moved[2]
        moved[2] = my + (side_f * SHEAR_SPEED) * rho
        moved[4] = moved[4] + (side_f * SHEAR_SPEED) * my + (0.5 * SHEAR_SPEED * SHEAR_SPEED) * rho
        for f in range(8):
            strip[f][z] = jnp.where(takes, moved[f], strip[f][z])
    main = advance(main, depth)
    strip = advance(strip, depth)

    inner = wide[:rows]
    for f in range(8):
        for z in range(depth):
            s = strip[f][z][:rows]
            new = jnp.where(inner < 4, turned(s, -8, 1), jnp.where(inner >= lanes - 8, s, main[f][z][:rows]))
            out_ref[f, z] = 0.5 * (state_ref[f, z] + new)

    at_sides(lambda copy: copy.wait_send())
    for copy in rims:
        copy.wait_send()


def on_device(nx, ny, state, offsets):
    fields, depth, rows, lanes = state.shape
    dma = pltpu.SemaphoreType.DMA
    plane = lambda *sizes: pltpu.VMEM((*sizes, lanes), jnp.float32)
    lines = 2 * fields * depth
    return pl.pallas_call(
        functools.partial(kernel, nx, ny),
        out_shape=jax.ShapeDtypeStruct(state.shape, state.dtype),
        in_specs=[
            pl.BlockSpec(memory_space=pltpu.SMEM),
            pl.BlockSpec(memory_space=pl.ANY),
        ],
        out_specs=pl.BlockSpec(memory_space=pltpu.VMEM),
        scratch_shapes=[
            plane(fields, depth, rows), plane(2, 8),
            plane(lines), plane(lines + 8), plane(lines + 8), plane(lines + 8),
            plane(8 * ny), plane(8 * ny), plane(3, 8), plane(3, 8), plane(rows * ny + 8),
            dma((2, ny)), dma((2, ny)), dma((2, 3)), dma((2, 3)), dma((2,)), dma((2,)),
            dma,
        ],
        compiler_params=pltpu.CompilerParams(collective_id=0, has_side_effects=True),
    )(offsets, state)


def solution(mesh):
    nx, ny = mesh.shape["gx"], mesh.shape["gy"]
    return jax.shard_map(
        functools.partial(on_device, nx, ny),
        mesh=mesh,
        in_specs=(P(None, None, "gy", "gx"), P()),
        out_specs=P(None, None, "gy", "gx"),
        check_vma=False,
    )
```

```python
import functools

import jax
import jax.numpy as jnp
from jax import lax
from jax.experimental import pallas as pl
from jax.experimental.pallas import tpu as pltpu
from jax.sharding import PartitionSpec as P

ADIABATIC = 5.0 / 3.0
SIGNAL_SPEED = 4.0
COURANT_RATIO = 0.06
SHEAR_SPEED = 1.5
MESH = pl.DeviceIdType.MESH


def turned(value, shift, axis):
    return pltpu.roll(value, shift % value.shape[axis], axis)


def advance(fields, depth):
    xm = lambda a: turned(a, 1, 1)
    xp = lambda a: turned(a, -1, 1)
    ym = lambda a: turned(a, 1, 0)
    yp = lambda a: turned(a, -1, 0)
    half_a = 0.5 * SIGNAL_SPEED
    levels = range(depth)
    below = lambda z: (z - 1) % depth
    above = lambda z: (z + 1) % depth

    cells, flux_z, emf = [], [], []
    for z in levels:
        rho, mx, my, mz, en, bx, by, bz = (fields[f][z] for f in range(8))
        cx = 0.5 * (bx + xp(bx))
        cy = 0.5 * (by + yp(by))
        cz = 0.5 * (bz + fields[7][above(z)])
        inv = 1.0 / rho
        vx, vy, vz = mx * inv, my * inv, mz * inv
        bsq = cx * cx + cy * cy + cz * cz
        pressure = (ADIABATIC - 1.0) * (en - 0.5 * (mx * vx + my * vy + mz * vz) - 0.5 * bsq)
        pt = pressure + 0.5 * bsq
        vb = vx * cx + vy * cy + vz * cz
        ept = en + pt
        mxy = mx * vy - cx * cy
        mxz = mx * vz - cx * cz
        myz = my * vz - cy * cz
        flux_x = (mx, mx * vx - cx * cx + pt, mxy, mxz, ept * vx - cx * vb)
        flux_y = (my, mxy, my * vy - cy * cy + pt, myz, ept * vy - cy * vb)
        flux_v = (mz, mxz, myz, mz * vz - cz * cz + pt, ept * vz - cz * vb)
        q = (rho, mx, my, mz, en)
        total = []
        ups, downs = [], []
        for f in range(5):
            aq = half_a * q[f]
            hx, hy, hz = 0.5 * flux_x[f], 0.5 * flux_y[f], 0.5 * flux_v[f]
            face_x = xm(hx + aq) + (hx - aq)
            face_y = ym(hy + aq) + (hy - aq)
            total.append((xp(face_x) - face_x) + (yp(face_y) - face_y))
            ups.append(hz + aq)
            downs.append(hz - aq)
        gz = 0.5 * (vx * cy - vy * cx)
        gx = 0.5 * (vy * cz - vz * cy)
        gy = 0.5 * (vx * cz - vz * cx)
        ax, ay, az = half_a * cx, half_a * cy, half_a * cz
        fx_by = xm(gz + ay) + (gz - ay)
        fy_bx = ym(ax - gz) - (gz + ax)
        ez = 0.25 * ((fy_bx + xm(fy_bx)) - (fx_by + ym(fx_by)))
        fy_bz = ym(gx + az) + (gx - az)
        fx_bz = xm(gy + az) + (gy - az)
        cells.append((q, total, ups, downs))
        emf.append((ez, fy_bz, fx_bz, ay - gx, gx + ay, ax - gy, gy + ax))

    ex, ey = [], []
    for z in levels:
        fz_by = emf[below(z)][3] - emf[z][4]
        fz_bx = emf[below(z)][5] - emf[z][6]
        ex.append(0.25 * ((fz_by + ym(fz_by)) - (emf[z][1] + emf[below(z)][1])))
        ey.append(0.25 * ((emf[z][2] + emf[below(z)][2]) - (fz_bx + xm(fz_bx))))

    face_z = [
        [cells[below(z)][2][f] + cells[z][3][f] for f in range(5)] for z in levels
    ]
    out = [[None] * depth for _ in range(8)]
    for z in levels:
        q, total, _, _ = cells[z]
        for f in range(5):
            change = total[f] + (face_z[above(z)][f] - face_z[z][f])
            out[f][z] = q[f] - COURANT_RATIO * change
        ez = emf[z][0]
        dz_ey = ey[above(z)] - ey[z]
        dz_ex = ex[above(z)] - ex[z]
        out[5][z] = fields[5][z] - COURANT_RATIO * ((yp(ez) - ez) - dz_ey)
        out[6][z] = fields[6][z] - COURANT_RATIO * (dz_ex - (xp(ez) - ez))
        out[7][z] = fields[7][z] - COURANT_RATIO * ((xp(ey[z]) - ey[z]) - (yp(ex[z]) - ex[z]))
    return out


def kernel(
    nx, ny, offsets_ref, input_ref, out_ref, state_ref, packs, rim_up, rim_down, rim_low, rim_high,
    gather_low, gather_high, halo_left, halo_right, joined,
    send_edge, recv_edge, send_side, recv_side, send_rim, recv_rim, load_sem,
):
    fields, depth, rows, lanes = state_ref.shape
    cx, cy = lax.axis_index("gx"), lax.axis_index("gy")
    up, down = lax.rem(cy + 1, ny), lax.rem(cy + ny - 1, ny)
    at_lower = cx == 0
    at_upper = cx == nx - 1
    at_edge = at_lower | at_upper
    lower_i = at_lower.astype(jnp.int32)
    upper_i = at_upper.astype(jnp.int32)
    lower_f = at_lower.astype(jnp.float32)
    upper_f = at_upper.astype(jnp.float32)
    opposite = jnp.where(at_lower, nx - 1, 0)
    near_rows = (down, cy, up)

    def around(action):
        def step(d, _):
            there = lax.rem(cy + d, ny)
            action(opposite, there)

            @pl.when(d < ny)
            def _():
                action(cx, there)

            return 0

        if ny > 16:
            lax.fori_loop(1, ny + 1, step, 0)
            return
        for d in range(1, ny + 1):
            there = lax.rem(cy + d, ny)
            action(opposite, there)
            if d < ny:
                action(cx, there)

    barrier = pltpu.get_barrier_semaphore()

    def greet(column, row):
        pl.semaphore_signal(barrier, inc=1, device_id=(column, row), device_id_type=MESH)

    load = pltpu.make_async_copy(input_ref, state_ref, load_sem)
    load.start()
    if nx == 2:
        around(greet)
        greetings = 2 * ny - 1
    else:

        @pl.when(at_edge)
        def _():
            around(greet)

        @pl.when(jnp.logical_not(at_edge))
        def _():
            greet(cx, up)
            greet(cx, down)

        @pl.when(jnp.logical_not(at_lower))
        def _():
            for row in near_rows:
                greet(cx - 1, row)

        @pl.when(jnp.logical_not(at_upper))
        def _():
            for row in near_rows:
                greet(cx + 1, row)

        greetings = jnp.where(at_edge, 2 * ny - 1 + 3, 2 + 6)

    lane = lax.broadcasted_iota(jnp.int32, (8, lanes), 1)
    sub = lane % 8
    part = lane // 8
    sublane = lax.broadcasted_iota(jnp.int32, (8, lanes), 0)
    swapped = lambda p: jnp.where(sub < 4, turned(p, -4, 1), turned(p, 4, 1))
    load.wait()
    tiles = []
    for t in (0, 8):
        packed = jnp.zeros((8, lanes), jnp.float32)
        for k in range(fields * depth):
            moved = turned(state_ref[k // depth, k % depth, t : t + 8, :], 8 * k + 4, 1)
            packed = jnp.where(part == k, moved, packed)
        tiles.append(packed)
    front = swapped(tiles[0])
    low = jnp.where(sub < 4, front, tiles[1])
    high = jnp.where(sub < 4, tiles[1], front)
    packs[0] = low
    packs[1] = high
    own_rows = pl.ds(pl.multiple_of(cy * 8, 8), 8)

    @pl.when(at_lower)
    def _():
        gather_low[own_rows, :] = low

    @pl.when(at_upper)
    def _():
        gather_high[own_rows, :] = high

    spots = []
    for k in range(fields * depth):
        f, z = k // depth, k % depth
        count = 3 if f == 6 else 2
        spots.append((spots[-1][0] + spots[-1][1] if spots else 0, count))
        rim_up[2 * k : 2 * k + 2, :] = state_ref[f, z, rows - 2 : rows, :]
        rim_down[spots[k][0] : spots[k][0] + count, :] = state_ref[f, z, 0:count, :]

    pl.semaphore_wait(barrier, greetings)

    def edge_copy(buffer, side, column, target, source):
        return pltpu.make_async_remote_copy(
            src_ref=packs.at[side],
            dst_ref=buffer.at[pl.ds(pl.multiple_of(source * 8, 8), 8), :],
            send_sem=send_edge.at[(column == cx).astype(jnp.int32), target],
            recv_sem=recv_edge.at[side, source],
            device_id=(column, target), device_id_type=MESH,
        )

    def side_copy(buffer, side, column, n):
        return pltpu.make_async_remote_copy(
            src_ref=packs.at[side], dst_ref=buffer.at[2 - n],
            send_sem=send_side.at[side, n], recv_sem=recv_side.at[side, 2 - n],
            device_id=(column, near_rows[n]), device_id_type=MESH,
        )

    def at_sides(method):
        @pl.when(at_lower)
        def _():
            around(lambda c, r: method(edge_copy(gather_low, 0, c, r, cy)))

        @pl.when(at_upper)
        def _():
            around(lambda c, r: method(edge_copy(gather_high, 1, c, r, cy)))

        @pl.when(jnp.logical_not(at_lower))
        def _():
            for n in range(3):
                method(side_copy(halo_right, 0, cx - 1, n))

        @pl.when(jnp.logical_not(at_upper))
        def _():
            for n in range(3):
                method(side_copy(halo_left, 1, cx + 1, n))

    def arrivals(wait):
        def from_edge(c, r):
            @pl.when(c == 0)
            def _():
                wait(edge_copy(gather_low, 0, c, r, r))

            @pl.when(c != 0)
            def _():
                wait(edge_copy(gather_high, 1, c, r, r))

        @pl.when(at_edge)
        def _():
            around(from_edge)

        @pl.when(jnp.logical_not(at_upper))
        def _():
            for n in range(3):
                wait(side_copy(halo_right, 0, cx + 1, 2 - n))

        @pl.when(jnp.logical_not(at_lower))
        def _():
            for n in range(3):
                wait(side_copy(halo_left, 1, cx - 1, 2 - n))

    rims = [
        pltpu.make_async_remote_copy(
            src_ref=rim_up, dst_ref=rim_low.at[pl.ds(8, 2 * fields * depth), :],
            send_sem=send_rim.at[0], recv_sem=recv_rim.at[0],
            device_id=(cx, up), device_id_type=MESH,
        ),
        pltpu.make_async_remote_copy(
            src_ref=rim_down, dst_ref=rim_high,
            send_sem=send_rim.at[1], recv_sem=recv_rim.at[1],
            device_id=(cx, down), device_id_type=MESH,
        ),
    ]
    for copy in rims:
        copy.start()
    at_sides(lambda copy: copy.start())
    for copy in rims:
        copy.wait_recv()

    height = rows + 8
    wide = lax.broadcasted_iota(jnp.int32, (height, lanes), 1)
    whole = []
    for f in range(fields):
        whole.append([])
        for z in range(depth):
            after, before = spots[f * depth + z][0], 2 * (f * depth + z) + 2
            edge = jnp.where(
                sublane < 4, rim_high[after : after + 8, :], rim_low[before : before + 8, :]
            )
            whole[f].append(jnp.concatenate([state_ref[f, z], edge], axis=0))
    main = advance(advance(whole, depth), depth)
    for f in range(fields):
        for z in range(depth):
            out_ref[f, z] = 0.5 * (state_ref[f, z] + main[f][z][:rows])

    arrivals(lambda copy: copy.wait_recv())

    def unfold(low, high):
        return jnp.where(sub < 4, low, high), swapped(jnp.where(sub < 4, high, low))

    total_rows = rows * ny

    def lay(block):
        a, b = unfold(gather_low[pl.ds(block * 8, 8), :], gather_high[pl.ds(block * 8, 8), :])
        joined[pl.ds(block * rows, 8), :] = a
        joined[pl.ds(block * rows + 8, 8), :] = b

    if ny > 16:
        lax.fori_loop(0, ny, lambda b, _: (lay(b), 0)[1], 0)
    else:
        for block in range(ny):
            lay(block)
    joined[total_rows : total_rows + 8, :] = joined[0:8, :]

    first, second = offsets_ref[0], offsets_ref[1]
    base = cy * rows

    def slab(shift):
        def part_at(j):
            return joined[pl.ds(lax.rem(base + shift + (j + 2 * total_rows), total_rows), 8), :]

        edge = jnp.where(sublane < 4, part_at(rows), part_at(-8))
        return [part_at(0), part_at(8), edge]

    field_of = part // depth

    def corrected(tiles, sign):
        along = jnp.where((field_of == 2) | (field_of == 4), sign * SHEAR_SPEED, 0.0)
        square = jnp.where(field_of == 4, 0.5 * SHEAR_SPEED * SHEAR_SPEED, 0.0)
        return [
            p + along * turned(p, 8 * 2 * depth, 1) + square * turned(p, 8 * 4 * depth, 1)
            for p in tiles
        ]

    side = lower_i - upper_i
    side_f = lower_f - upper_f
    sheared = corrected(slab(side * first), side_f)
    far = slab(side * second)
    near = corrected(slab(side * (second - first)), -side_f)
    beside = [unfold(halo_right[n], halo_left[n]) for n in range(3)]
    plain = [beside[1][0], beside[1][1], jnp.where(sublane < 4, beside[2][0], beside[0][1])]
    is_low = sub < 4
    from_shear = (is_low & at_upper) | (jnp.logical_not(is_low) & at_lower)
    ghosts = [jnp.where(from_shear, a, b) for a, b in zip(sheared, plain)]
    joint = [swapped(jnp.where(is_low == at_upper, a, b)) for a, b in zip(far, near)]

    stack = lambda tiles: jnp.concatenate(tiles, axis=0)
    ghosts, joint = stack(ghosts), stack(joint)
    strip = []
    for f in range(fields):
        strip.append([])
        for z in range(depth):
            k = f * depth + z
            after, before = spots[k][0], 2 * k + 2
            edge = jnp.where(
                sublane < 4, rim_high[after : after + 8, :], rim_low[before : before + 8, :]
            )
            m = jnp.concatenate([state_ref[f, z], edge], axis=0)
            s = jnp.where(wide < 40, turned(m, 8, 1), m)
            s = jnp.where(wide < 8, turned(ghosts, -8 * k, 1), s)
            s = jnp.where((wide >= 40) & (wide < 48), turned(joint, 40 - 8 * k, 1), s)
            strip[f].append(s)

    strip = advance(strip, depth)
    back = jnp.where(at_lower, lanes - 36, lanes - 44)
    takes = ((wide == 7) & at_lower) | ((wide < 2) & at_upper)
    for z in range(depth):
        moved = [pltpu.roll(strip[f][z], back, 1) for f in range(8)]
        rho, my = moved[0], moved[2]
        moved[2] = my + (side_f * SHEAR_SPEED) * rho
        moved[4] = moved[4] + (side_f * SHEAR_SPEED) * my + (0.5 * SHEAR_SPEED * SHEAR_SPEED) * rho
        for f in range(8):
            strip[f][z] = jnp.where(takes, moved[f], strip[f][z])
    strip = advance(strip, depth)

    inner = wide[:rows]
    for f in range(8):
        for z in range(depth):
            s = strip[f][z][:rows]
            new = 0.5 * (state_ref[f, z] + jnp.where(inner < 4, turned(s, -8, 1), s))
            keep = (inner >= 4) & (inner < lanes - 8)
            out_ref[f, z] = jnp.where(keep, out_ref[f, z], new)

    at_sides(lambda copy: copy.wait_send())
    for copy in rims:
        copy.wait_send()


def on_device(nx, ny, state, offsets):
    fields, depth, rows, lanes = state.shape
    dma = pltpu.SemaphoreType.DMA
    plane = lambda *sizes: pltpu.VMEM((*sizes, lanes), jnp.float32)
    lines = 2 * fields * depth
    return pl.pallas_call(
        functools.partial(kernel, nx, ny),
        out_shape=jax.ShapeDtypeStruct(state.shape, state.dtype),
        in_specs=[
            pl.BlockSpec(memory_space=pltpu.SMEM),
            pl.BlockSpec(memory_space=pl.ANY),
        ],
        out_specs=pl.BlockSpec(memory_space=pltpu.VMEM),
        scratch_shapes=[
            plane(fields, depth, rows), plane(2, 8),
            plane(lines), plane(lines + 8), plane(lines + 8), plane(lines + 8),
            plane(8 * ny), plane(8 * ny), plane(3, 8), plane(3, 8), plane(rows * ny + 8),
            dma((2, ny)), dma((2, ny)), dma((2, 3)), dma((2, 3)), dma((2,)), dma((2,)),
            dma,
        ],
        compiler_params=pltpu.CompilerParams(collective_id=0, has_side_effects=True),
    )(offsets, state)


def solution(mesh):
    nx, ny = mesh.shape["gx"], mesh.shape["gy"]
    return jax.shard_map(
        functools.partial(on_device, nx, ny),
        mesh=mesh,
        in_specs=(P(None, None, "gy", "gx"), P()),
        out_specs=P(None, None, "gy", "gx"),
        check_vma=False,
    )
```

```python
import functools

import jax
import jax.numpy as jnp
from jax import lax
from jax.experimental import pallas as pl
from jax.experimental.pallas import tpu as pltpu
from jax.sharding import PartitionSpec as P

ADIABATIC = 5.0 / 3.0
SIGNAL_SPEED = 4.0
COURANT_RATIO = 0.06
SHEAR_SPEED = 1.5
MESH = pl.DeviceIdType.MESH


def turned(value, shift, axis):
    return pltpu.roll(value, shift % value.shape[axis], axis)


def advance(fields, depth):
    xm = lambda a: turned(a, 1, 1)
    xp = lambda a: turned(a, -1, 1)
    ym = lambda a: turned(a, 1, 0)
    yp = lambda a: turned(a, -1, 0)
    half_a = 0.5 * SIGNAL_SPEED
    levels = range(depth)
    below = lambda z: (z - 1) % depth
    above = lambda z: (z + 1) % depth

    cells, flux_z, emf = [], [], []
    for z in levels:
        rho, mx, my, mz, en, bx, by, bz = (fields[f][z] for f in range(8))
        cx = 0.5 * (bx + xp(bx))
        cy = 0.5 * (by + yp(by))
        cz = 0.5 * (bz + fields[7][above(z)])
        inv = 1.0 / rho
        vx, vy, vz = mx * inv, my * inv, mz * inv
        bsq = cx * cx + cy * cy + cz * cz
        pressure = (ADIABATIC - 1.0) * (en - 0.5 * (mx * vx + my * vy + mz * vz) - 0.5 * bsq)
        pt = pressure + 0.5 * bsq
        vb = vx * cx + vy * cy + vz * cz
        ept = en + pt
        mxy = mx * vy - cx * cy
        mxz = mx * vz - cx * cz
        myz = my * vz - cy * cz
        flux_x = (mx, mx * vx - cx * cx + pt, mxy, mxz, ept * vx - cx * vb)
        flux_y = (my, mxy, my * vy - cy * cy + pt, myz, ept * vy - cy * vb)
        flux_v = (mz, mxz, myz, mz * vz - cz * cz + pt, ept * vz - cz * vb)
        q = (rho, mx, my, mz, en)
        total = []
        ups, downs = [], []
        for f in range(5):
            aq = half_a * q[f]
            hx, hy, hz = 0.5 * flux_x[f], 0.5 * flux_y[f], 0.5 * flux_v[f]
            face_x = xm(hx + aq) + (hx - aq)
            face_y = ym(hy + aq) + (hy - aq)
            total.append((xp(face_x) - face_x) + (yp(face_y) - face_y))
            ups.append(hz + aq)
            downs.append(hz - aq)
        gz = 0.5 * (vx * cy - vy * cx)
        gx = 0.5 * (vy * cz - vz * cy)
        gy = 0.5 * (vx * cz - vz * cx)
        ax, ay, az = half_a * cx, half_a * cy, half_a * cz
        fx_by = xm(gz + ay) + (gz - ay)
        fy_bx = ym(ax - gz) - (gz + ax)
        ez = 0.25 * ((fy_bx + xm(fy_bx)) - (fx_by + ym(fx_by)))
        fy_bz = ym(gx + az) + (gx - az)
        fx_bz = xm(gy + az) + (gy - az)
        cells.append((q, total, ups, downs))
        emf.append((ez, fy_bz, fx_bz, ay - gx, gx + ay, ax - gy, gy + ax))

    ex, ey = [], []
    for z in levels:
        fz_by = emf[below(z)][3] - emf[z][4]
        fz_bx = emf[below(z)][5] - emf[z][6]
        ex.append(0.25 * ((fz_by + ym(fz_by)) - (emf[z][1] + emf[below(z)][1])))
        ey.append(0.25 * ((emf[z][2] + emf[below(z)][2]) - (fz_bx + xm(fz_bx))))

    face_z = [
        [cells[below(z)][2][f] + cells[z][3][f] for f in range(5)] for z in levels
    ]
    out = [[None] * depth for _ in range(8)]
    for z in levels:
        q, total, _, _ = cells[z]
        for f in range(5):
            change = total[f] + (face_z[above(z)][f] - face_z[z][f])
            out[f][z] = q[f] - COURANT_RATIO * change
        ez = emf[z][0]
        dz_ey = ey[above(z)] - ey[z]
        dz_ex = ex[above(z)] - ex[z]
        out[5][z] = fields[5][z] - COURANT_RATIO * ((yp(ez) - ez) - dz_ey)
        out[6][z] = fields[6][z] - COURANT_RATIO * (dz_ex - (xp(ez) - ez))
        out[7][z] = fields[7][z] - COURANT_RATIO * ((xp(ey[z]) - ey[z]) - (yp(ex[z]) - ex[z]))
    return out


def kernel(
    nx, ny, offsets_ref, input_ref, out_ref, state_ref, packs, rim_up, rim_down, rim_low, rim_high,
    gather_low, gather_high, halo_left, halo_right, joined,
    send_edge, recv_edge, send_side, recv_side, send_rim, recv_rim, load_sem,
):
    fields, depth, rows, lanes = state_ref.shape
    cx, cy = lax.axis_index("gx"), lax.axis_index("gy")
    up, down = lax.rem(cy + 1, ny), lax.rem(cy + ny - 1, ny)
    at_lower = cx == 0
    at_upper = cx == nx - 1
    at_edge = at_lower | at_upper
    lower_i = at_lower.astype(jnp.int32)
    upper_i = at_upper.astype(jnp.int32)
    lower_f = at_lower.astype(jnp.float32)
    upper_f = at_upper.astype(jnp.float32)
    opposite = jnp.where(at_lower, nx - 1, 0)
    near_rows = (down, cy, up)

    def around(action):
        def step(d, _):
            there = lax.rem(cy + d, ny)
            action(opposite, there)

            @pl.when(d < ny)
            def _():
                action(cx, there)

            return 0

        if ny > 16:
            lax.fori_loop(1, ny + 1, step, 0)
            return
        for d in range(1, ny + 1):
            there = lax.rem(cy + d, ny)
            action(opposite, there)
            if d < ny:
                action(cx, there)

    barrier = pltpu.get_barrier_semaphore()

    def greet(column, row):
        pl.semaphore_signal(barrier, inc=1, device_id=(column, row), device_id_type=MESH)

    load = pltpu.make_async_copy(input_ref, state_ref, load_sem)
    load.start()
    if nx == 2:
        around(greet)
        greetings = 2 * ny - 1
    else:

        @pl.when(at_edge)
        def _():
            around(greet)

        @pl.when(jnp.logical_not(at_edge))
        def _():
            greet(cx, up)
            greet(cx, down)

        @pl.when(jnp.logical_not(at_lower))
        def _():
            for row in near_rows:
                greet(cx - 1, row)

        @pl.when(jnp.logical_not(at_upper))
        def _():
            for row in near_rows:
                greet(cx + 1, row)

        greetings = jnp.where(at_edge, 2 * ny - 1 + 3, 2 + 6)

    lane = lax.broadcasted_iota(jnp.int32, (8, lanes), 1)
    sub = lane % 8
    part = lane // 8
    sublane = lax.broadcasted_iota(jnp.int32, (8, lanes), 0)
    swapped = lambda p: jnp.where(sub < 4, turned(p, -4, 1), turned(p, 4, 1))
    load.wait()
    tiles = []
    for t in (0, 8):
        packed = jnp.zeros((8, lanes), jnp.float32)
        for k in range(fields * depth):
            moved = turned(state_ref[k // depth, k % depth, t : t + 8, :], 8 * k + 4, 1)
            packed = jnp.where(part == k, moved, packed)
        tiles.append(packed)
    front = swapped(tiles[0])
    low = jnp.where(sub < 4, front, tiles[1])
    high = jnp.where(sub < 4, tiles[1], front)
    packs[0] = low
    packs[1] = high
    own_rows = pl.ds(pl.multiple_of(cy * 8, 8), 8)

    @pl.when(at_lower)
    def _():
        gather_low[own_rows, :] = low

    @pl.when(at_upper)
    def _():
        gather_high[own_rows, :] = high

    spots = []
    for k in range(fields * depth):
        f, z = k // depth, k % depth
        count = 3 if f == 6 else 2
        spots.append((spots[-1][0] + spots[-1][1] if spots else 0, count))
        rim_up[2 * k : 2 * k + 2, :] = state_ref[f, z, rows - 2 : rows, :]
        rim_down[spots[k][0] : spots[k][0] + count, :] = state_ref[f, z, 0:count, :]

    pl.semaphore_wait(barrier, greetings)

    def edge_copy(buffer, side, column, target, source):
        return pltpu.make_async_remote_copy(
            src_ref=packs.at[side],
            dst_ref=buffer.at[pl.ds(pl.multiple_of(source * 8, 8), 8), :],
            send_sem=send_edge.at[(column == cx).astype(jnp.int32), target],
            recv_sem=recv_edge.at[side, source],
            device_id=(column, target), device_id_type=MESH,
        )

    def side_copy(buffer, side, column, n):
        return pltpu.make_async_remote_copy(
            src_ref=packs.at[side], dst_ref=buffer.at[2 - n],
            send_sem=send_side.at[side, n], recv_sem=recv_side.at[side, 2 - n],
            device_id=(column, near_rows[n]), device_id_type=MESH,
        )

    def at_sides(method):
        @pl.when(at_lower)
        def _():
            around(lambda c, r: method(edge_copy(gather_low, 0, c, r, cy)))

        @pl.when(at_upper)
        def _():
            around(lambda c, r: method(edge_copy(gather_high, 1, c, r, cy)))

        @pl.when(jnp.logical_not(at_lower))
        def _():
            for n in range(3):
                method(side_copy(halo_right, 0, cx - 1, n))

        @pl.when(jnp.logical_not(at_upper))
        def _():
            for n in range(3):
                method(side_copy(halo_left, 1, cx + 1, n))

    def arrivals(wait):
        def from_edge(c, r):
            @pl.when(c == 0)
            def _():
                wait(edge_copy(gather_low, 0, c, r, r))

            @pl.when(c != 0)
            def _():
                wait(edge_copy(gather_high, 1, c, r, r))

        @pl.when(at_edge)
        def _():
            around(from_edge)

        @pl.when(jnp.logical_not(at_upper))
        def _():
            for n in range(3):
                wait(side_copy(halo_right, 0, cx + 1, 2 - n))

        @pl.when(jnp.logical_not(at_lower))
        def _():
            for n in range(3):
                wait(side_copy(halo_left, 1, cx - 1, 2 - n))

    rims = [
        pltpu.make_async_remote_copy(
            src_ref=rim_up, dst_ref=rim_low.at[pl.ds(8, 2 * fields * depth), :],
            send_sem=send_rim.at[0], recv_sem=recv_rim.at[0],
            device_id=(cx, up), device_id_type=MESH,
        ),
        pltpu.make_async_remote_copy(
            src_ref=rim_down, dst_ref=rim_high,
            send_sem=send_rim.at[1], recv_sem=recv_rim.at[1],
            device_id=(cx, down), device_id_type=MESH,
        ),
    ]
    for copy in rims:
        copy.start()
    at_sides(lambda copy: copy.start())
    for copy in rims:
        copy.wait_recv()

    height = rows + 8
    wide = lax.broadcasted_iota(jnp.int32, (height, lanes), 1)
    whole = []
    for f in range(fields):
        whole.append([])
        for z in range(depth):
            after, before = spots[f * depth + z][0], 2 * (f * depth + z) + 2
            edge = jnp.where(
                sublane < 4, rim_high[after : after + 8, :], rim_low[before : before + 8, :]
            )
            whole[f].append(jnp.concatenate([state_ref[f, z], edge], axis=0))
    main = advance(advance(whole, depth), depth)
    for f in range(fields):
        for z in range(depth):
            out_ref[f, z] = 0.5 * (state_ref[f, z] + main[f][z][:rows])

    arrivals(lambda copy: copy.wait_recv())

    def unfold(low, high):
        return jnp.where(sub < 4, low, high), swapped(jnp.where(sub < 4, high, low))

    total_rows = rows * ny

    def lay(block):
        a, b = unfold(gather_low[pl.ds(block * 8, 8), :], gather_high[pl.ds(block * 8, 8), :])
        joined[pl.ds(block * rows, 8), :] = a
        joined[pl.ds(block * rows + 8, 8), :] = b

    if ny > 16:
        lax.fori_loop(0, ny, lambda b, _: (lay(b), 0)[1], 0)
    else:
        for block in range(ny):
            lay(block)
    joined[total_rows : total_rows + 8, :] = joined[0:8, :]

    first, second = offsets_ref[0], offsets_ref[1]
    base = cy * rows

    def slab(shift):
        def part_at(j):
            return joined[pl.ds(lax.rem(base + shift + (j + 2 * total_rows), total_rows), 8), :]

        edge = jnp.where(sublane < 4, part_at(rows), part_at(-8))
        return [part_at(0), part_at(8), edge]

    field_of = part // depth

    def corrected(tiles, sign):
        along = jnp.where((field_of == 2) | (field_of == 4), sign * SHEAR_SPEED, 0.0)
        square = jnp.where(field_of == 4, 0.5 * SHEAR_SPEED * SHEAR_SPEED, 0.0)
        return [
            p + along * turned(p, 8 * 2 * depth, 1) + square * turned(p, 8 * 4 * depth, 1)
            for p in tiles
        ]

    side = lower_i - upper_i
    side_f = lower_f - upper_f
    sheared = corrected(slab(side * first), side_f)
    far = slab(side * second)
    near = corrected(slab(side * (second - first)), -side_f)
    beside = [unfold(halo_right[n], halo_left[n]) for n in range(3)]
    plain = [beside[1][0], beside[1][1], jnp.where(sublane < 4, beside[2][0], beside[0][1])]
    is_low = sub < 4
    from_shear = (is_low & at_upper) | (jnp.logical_not(is_low) & at_lower)
    ghosts = [jnp.where(from_shear, a, b) for a, b in zip(sheared, plain)]
    joint = [swapped(jnp.where(is_low == at_upper, a, b)) for a, b in zip(far, near)]

    stack = lambda tiles: jnp.concatenate(tiles, axis=0)
    ghosts, joint = stack(ghosts), stack(joint)
    strip = []
    for f in range(fields):
        strip.append([])
        for z in range(depth):
            k = f * depth + z
            after, before = spots[k][0], 2 * k + 2
            edge = jnp.where(
                sublane < 4, rim_high[after : after + 8, :], rim_low[before : before + 8, :]
            )
            m = jnp.concatenate([state_ref[f, z], edge], axis=0)
            s = jnp.where(wide < 40, turned(m, 8, 1), m)
            s = jnp.where(wide < 8, turned(ghosts, -8 * k, 1), s)
            s = jnp.where((wide >= 40) & (wide < 48), turned(joint, 40 - 8 * k, 1), s)
            strip[f].append(s)

    strip = advance(strip, depth)
    back = jnp.where(at_lower, lanes - 36, lanes - 44)
    takes = ((wide == 7) & at_lower) | ((wide < 2) & at_upper)
    for z in range(depth):
        moved = [pltpu.roll(strip[f][z], back, 1) for f in range(8)]
        rho, my = moved[0], moved[2]
        moved[2] = my + (side_f * SHEAR_SPEED) * rho
        moved[4] = moved[4] + (side_f * SHEAR_SPEED) * my + (0.5 * SHEAR_SPEED * SHEAR_SPEED) * rho
        for f in range(8):
            strip[f][z] = jnp.where(takes, moved[f], strip[f][z])
    strip = advance(strip, depth)

    inner = wide[:rows]
    for f in range(8):
        for z in range(depth):
            s = strip[f][z][:rows]
            new = 0.5 * (state_ref[f, z] + jnp.where(inner < 4, turned(s, -8, 1), s))
            keep = (inner >= 4) & (inner < lanes - 8)
            out_ref[f, z] = jnp.where(keep, out_ref[f, z], new)

    at_sides(lambda copy: copy.wait_send())
    for copy in rims:
        copy.wait_send()


def write_out(new_ref, out_ref, sem):
    copy = pltpu.make_async_copy(new_ref, out_ref, sem)
    copy.start()
    copy.wait()


def on_device(nx, ny, state, offsets):
    fields, depth, rows, lanes = state.shape
    dma = pltpu.SemaphoreType.DMA
    plane = lambda *sizes: pltpu.VMEM((*sizes, lanes), jnp.float32)
    lines = 2 * fields * depth
    new = pl.pallas_call(
        functools.partial(kernel, nx, ny),
        out_shape=pltpu.VMEM(state.shape, state.dtype),
        in_specs=[
            pl.BlockSpec(memory_space=pltpu.SMEM),
            pl.BlockSpec(memory_space=pl.ANY),
        ],
        out_specs=pl.BlockSpec(memory_space=pltpu.VMEM),
        scratch_shapes=[
            plane(fields, depth, rows), plane(2, 8),
            plane(lines), plane(lines + 8), plane(lines + 8), plane(lines + 8),
            plane(8 * ny), plane(8 * ny), plane(3, 8), plane(3, 8), plane(rows * ny + 8),
            dma((2, ny)), dma((2, ny)), dma((2, 3)), dma((2, 3)), dma((2,)), dma((2,)),
            dma,
        ],
        compiler_params=pltpu.CompilerParams(
            collective_id=0, has_side_effects=True
        ),
    )(offsets, state)
    return pl.pallas_call(
        write_out,
        out_shape=jax.ShapeDtypeStruct(state.shape, state.dtype),
        in_specs=[pl.BlockSpec(memory_space=pltpu.VMEM)],
        out_specs=pl.BlockSpec(memory_space=pl.ANY),
        scratch_shapes=[dma],
        compiler_params=pltpu.CompilerParams(vmem_limit_bytes=1 << 20),
    )(new)


def solution(mesh):
    nx, ny = mesh.shape["gx"], mesh.shape["gy"]
    return jax.shard_map(
        functools.partial(on_device, nx, ny),
        mesh=mesh,
        in_specs=(P(None, None, "gy", "gx"), P()),
        out_specs=P(None, None, "gy", "gx"),
        check_vma=False,
    )
```

```python
import functools

import jax
import jax.numpy as jnp
from jax import lax
from jax.experimental import pallas as pl
from jax.experimental.pallas import tpu as pltpu
from jax.sharding import PartitionSpec as P

ADIABATIC = 5.0 / 3.0
SIGNAL_SPEED = 4.0
COURANT_RATIO = 0.06
SHEAR_SPEED = 1.5
MESH = pl.DeviceIdType.MESH


def turned(value, shift, axis):
    return pltpu.roll(value, shift % value.shape[axis], axis)


def advance(fields, depth):
    xm = lambda a: turned(a, 1, 1)
    xp = lambda a: turned(a, -1, 1)
    ym = lambda a: turned(a, 1, 0)
    yp = lambda a: turned(a, -1, 0)
    half_a = 0.5 * SIGNAL_SPEED
    levels = range(depth)
    below = lambda z: (z - 1) % depth
    above = lambda z: (z + 1) % depth

    cells, flux_z, emf = [], [], []
    for z in levels:
        rho, mx, my, mz, en, bx, by, bz = (fields[f][z] for f in range(8))
        cx = 0.5 * (bx + xp(bx))
        cy = 0.5 * (by + yp(by))
        cz = 0.5 * (bz + fields[7][above(z)])
        inv = 1.0 / rho
        vx, vy, vz = mx * inv, my * inv, mz * inv
        bsq = cx * cx + cy * cy + cz * cz
        pressure = (ADIABATIC - 1.0) * (en - 0.5 * (mx * vx + my * vy + mz * vz) - 0.5 * bsq)
        pt = pressure + 0.5 * bsq
        vb = vx * cx + vy * cy + vz * cz
        ept = en + pt
        mxy = mx * vy - cx * cy
        mxz = mx * vz - cx * cz
        myz = my * vz - cy * cz
        flux_x = (mx, mx * vx - cx * cx + pt, mxy, mxz, ept * vx - cx * vb)
        flux_y = (my, mxy, my * vy - cy * cy + pt, myz, ept * vy - cy * vb)
        flux_v = (mz, mxz, myz, mz * vz - cz * cz + pt, ept * vz - cz * vb)
        q = (rho, mx, my, mz, en)
        total = []
        ups, downs = [], []
        for f in range(5):
            aq = half_a * q[f]
            hx, hy, hz = 0.5 * flux_x[f], 0.5 * flux_y[f], 0.5 * flux_v[f]
            face_x = xm(hx + aq) + (hx - aq)
            face_y = ym(hy + aq) + (hy - aq)
            total.append((xp(face_x) - face_x) + (yp(face_y) - face_y))
            ups.append(hz + aq)
            downs.append(hz - aq)
        gz = 0.5 * (vx * cy - vy * cx)
        gx = 0.5 * (vy * cz - vz * cy)
        gy = 0.5 * (vx * cz - vz * cx)
        ax, ay, az = half_a * cx, half_a * cy, half_a * cz
        fx_by = xm(gz + ay) + (gz - ay)
        fy_bx = ym(ax - gz) - (gz + ax)
        ez = 0.25 * ((fy_bx + xm(fy_bx)) - (fx_by + ym(fx_by)))
        fy_bz = ym(gx + az) + (gx - az)
        fx_bz = xm(gy + az) + (gy - az)
        cells.append((q, total, ups, downs))
        emf.append((ez, fy_bz, fx_bz, ay - gx, gx + ay, ax - gy, gy + ax))

    ex, ey = [], []
    for z in levels:
        fz_by = emf[below(z)][3] - emf[z][4]
        fz_bx = emf[below(z)][5] - emf[z][6]
        ex.append(0.25 * ((fz_by + ym(fz_by)) - (emf[z][1] + emf[below(z)][1])))
        ey.append(0.25 * ((emf[z][2] + emf[below(z)][2]) - (fz_bx + xm(fz_bx))))

    face_z = [
        [cells[below(z)][2][f] + cells[z][3][f] for f in range(5)] for z in levels
    ]
    out = [[None] * depth for _ in range(8)]
    for z in levels:
        q, total, _, _ = cells[z]
        for f in range(5):
            change = total[f] + (face_z[above(z)][f] - face_z[z][f])
            out[f][z] = q[f] - COURANT_RATIO * change
        ez = emf[z][0]
        dz_ey = ey[above(z)] - ey[z]
        dz_ex = ex[above(z)] - ex[z]
        out[5][z] = fields[5][z] - COURANT_RATIO * ((yp(ez) - ez) - dz_ey)
        out[6][z] = fields[6][z] - COURANT_RATIO * (dz_ex - (xp(ez) - ez))
        out[7][z] = fields[7][z] - COURANT_RATIO * ((xp(ey[z]) - ey[z]) - (yp(ex[z]) - ex[z]))
    return out


def kernel(
    nx, ny, offsets_ref, input_ref, out_ref, state_ref, packs, rim_up, rim_down, rim_low, rim_high,
    gather, halo, joined,
    send_edge, recv_edge, send_side, recv_side, send_rim, recv_rim, load_sem,
):
    fields, depth, rows, lanes = state_ref.shape
    cx, cy = lax.axis_index("gx"), lax.axis_index("gy")
    up, down = lax.rem(cy + 1, ny), lax.rem(cy + ny - 1, ny)
    at_lower = cx == 0
    at_upper = cx == nx - 1
    at_edge = at_lower | at_upper
    lower_i = at_lower.astype(jnp.int32)
    upper_i = at_upper.astype(jnp.int32)
    lower_f = at_lower.astype(jnp.float32)
    upper_f = at_upper.astype(jnp.float32)
    opposite = jnp.where(at_lower, nx - 1, 0)
    near_rows = (down, cy, up)
    outer = jnp.where(at_lower, 0, 1)
    inner_side = 1 - outer

    def around(action):
        def step(d, _):
            there = lax.rem(cy + d, ny)
            action(opposite, there)

            @pl.when(d < ny)
            def _():
                action(cx, there)

            return 0

        if ny > 16:
            lax.fori_loop(1, ny + 1, step, 0)
            return
        for d in range(1, ny + 1):
            there = lax.rem(cy + d, ny)
            action(opposite, there)
            if d < ny:
                action(cx, there)

    barrier = pltpu.get_barrier_semaphore()

    def greet(column, row):
        pl.semaphore_signal(barrier, inc=1, device_id=(column, row), device_id_type=MESH)

    load = pltpu.make_async_copy(input_ref, state_ref, load_sem)
    load.start()
    if nx == 2:
        around(greet)
        greetings = 2 * ny - 1
    else:

        @pl.when(at_edge)
        def _():
            around(greet)

        @pl.when(jnp.logical_not(at_edge))
        def _():
            greet(cx, up)
            greet(cx, down)

        @pl.when(jnp.logical_not(at_lower))
        def _():
            for row in near_rows:
                greet(cx - 1, row)

        @pl.when(jnp.logical_not(at_upper))
        def _():
            for row in near_rows:
                greet(cx + 1, row)

        greetings = jnp.where(at_edge, 2 * ny - 1 + 3, 2 + 6)

    lane = lax.broadcasted_iota(jnp.int32, (8, lanes), 1)
    sub = lane % 8
    part = lane // 8
    sublane = lax.broadcasted_iota(jnp.int32, (8, lanes), 0)
    swapped = lambda p: jnp.where(sub < 4, turned(p, -4, 1), turned(p, 4, 1))
    load.wait()
    tiles = []
    for t in (0, 8):
        packed = jnp.zeros((8, lanes), jnp.float32)
        for k in range(fields * depth):
            moved = turned(state_ref[k // depth, k % depth, t : t + 8, :], 8 * k + 4, 1)
            packed = jnp.where(part == k, moved, packed)
        tiles.append(packed)
    front = swapped(tiles[0])
    low = jnp.where(sub < 4, front, tiles[1])
    high = jnp.where(sub < 4, tiles[1], front)
    packs[0] = low
    packs[1] = high
    own_rows = pl.ds(pl.multiple_of(cy * 8, 8), 8)

    gather[outer, own_rows, :] = jnp.where(at_lower, low, high)

    spots = []
    for k in range(fields * depth):
        f, z = k // depth, k % depth
        count = 3 if f == 6 else 2
        spots.append((spots[-1][0] + spots[-1][1] if spots else 0, count))
        rim_up[2 * k : 2 * k + 2, :] = state_ref[f, z, rows - 2 : rows, :]
        rim_down[spots[k][0] : spots[k][0] + count, :] = state_ref[f, z, 0:count, :]

    pl.semaphore_wait(barrier, greetings)

    def edge_copy(column, target):
        return pltpu.make_async_remote_copy(
            src_ref=packs.at[outer], dst_ref=gather.at[outer, own_rows, :],
            send_sem=send_edge, recv_sem=recv_edge.at[outer],
            device_id=(column, target), device_id_type=MESH,
        )

    def edge_wait(buffer, blocks, sem):
        area = buffer.at[pl.ds(0, 8 * blocks), :]
        pltpu.make_async_copy(area, area, sem).wait()

    def side_copy(side, column, n):
        return pltpu.make_async_remote_copy(
            src_ref=packs.at[side], dst_ref=halo.at[side, 2 - n],
            send_sem=send_side.at[side, n], recv_sem=recv_side.at[side, 2 - n],
            device_id=(column, near_rows[n]), device_id_type=MESH,
        )

    def at_edges(action):
        if nx == 2:
            action()
        else:
            pl.when(at_edge)(action)

    def sides(action, arriving):
        if nx == 2:
            for n in range(3):
                action(side_copy(outer if arriving else inner_side, opposite, n))
            return
        for side, column, absent in ((0, cx - 1, at_lower), (1, cx + 1, at_upper)):
            if arriving:
                column, absent = (cx + 1, at_upper) if side == 0 else (cx - 1, at_lower)

            @pl.when(jnp.logical_not(absent))
            def _():
                for n in range(3):
                    action(side_copy(side, column, n))

    def start_edges():
        around(lambda column, row: edge_copy(column, row).start())

    def await_edges():
        edge_wait(gather.at[outer], ny - 1, recv_edge.at[outer])
        edge_wait(gather.at[inner_side], ny, recv_edge.at[inner_side])

    def await_sent_edges():
        edge_wait(joined, 2 * ny - 1, send_edge)

    rims = [
        pltpu.make_async_remote_copy(
            src_ref=rim_up, dst_ref=rim_low.at[pl.ds(8, 2 * fields * depth), :],
            send_sem=send_rim.at[0], recv_sem=recv_rim.at[0],
            device_id=(cx, up), device_id_type=MESH,
        ),
        pltpu.make_async_remote_copy(
            src_ref=rim_down, dst_ref=rim_high,
            send_sem=send_rim.at[1], recv_sem=recv_rim.at[1],
            device_id=(cx, down), device_id_type=MESH,
        ),
    ]
    for copy in rims:
        copy.start()
    at_edges(start_edges)
    sides(lambda copy: copy.start(), False)
    for copy in rims:
        copy.wait_recv()

    height = rows + 8
    wide = lax.broadcasted_iota(jnp.int32, (height, lanes), 1)
    whole = []
    for f in range(fields):
        whole.append([])
        for z in range(depth):
            after, before = spots[f * depth + z][0], 2 * (f * depth + z) + 2
            edge = jnp.where(
                sublane < 4, rim_high[after : after + 8, :], rim_low[before : before + 8, :]
            )
            whole[f].append(jnp.concatenate([state_ref[f, z], edge], axis=0))
    main = advance(advance(whole, depth), depth)
    for f in range(fields):
        for z in range(depth):
            out_ref[f, z] = 0.5 * (state_ref[f, z] + main[f][z][:rows])

    own_part = [
        [jnp.where(wide < 40, turned(m, 8, 1), m) for m in levels] for levels in whole
    ]

    sides(lambda copy: copy.wait_recv(), True)
    at_edges(await_edges)

    def unfold(low, high):
        return jnp.where(sub < 4, low, high), swapped(jnp.where(sub < 4, high, low))

    total_rows = rows * ny

    def lay(block):
        a, b = unfold(gather[0, pl.ds(block * 8, 8), :], gather[1, pl.ds(block * 8, 8), :])
        joined[pl.ds(block * rows, 8), :] = a
        joined[pl.ds(block * rows + 8, 8), :] = b

    if ny > 16:
        lax.fori_loop(0, ny, lambda b, _: (lay(b), 0)[1], 0)
    else:
        for block in range(ny):
            lay(block)
    joined[total_rows : total_rows + 8, :] = joined[0:8, :]

    first, second = offsets_ref[0], offsets_ref[1]
    base = cy * rows

    def slab(shift):
        def part_at(j):
            return joined[pl.ds(lax.rem(base + shift + (j + 2 * total_rows), total_rows), 8), :]

        edge = jnp.where(sublane < 4, part_at(rows), part_at(-8))
        return [part_at(0), part_at(8), edge]

    field_of = part // depth

    def corrected(tiles, sign):
        along = jnp.where((field_of == 2) | (field_of == 4), sign * SHEAR_SPEED, 0.0)
        square = jnp.where(field_of == 4, 0.5 * SHEAR_SPEED * SHEAR_SPEED, 0.0)
        return [
            p + along * turned(p, 8 * 2 * depth, 1) + square * turned(p, 8 * 4 * depth, 1)
            for p in tiles
        ]

    side = lower_i - upper_i
    side_f = lower_f - upper_f
    sheared = corrected(slab(side * first), side_f)
    far = slab(side * second)
    near = corrected(slab(side * (second - first)), -side_f)
    beside = [unfold(halo[0, n], halo[1, n]) for n in range(3)]
    plain = [beside[1][0], beside[1][1], jnp.where(sublane < 4, beside[2][0], beside[0][1])]
    is_low = sub < 4
    from_shear = (is_low & at_upper) | (jnp.logical_not(is_low) & at_lower)
    ghosts = [jnp.where(from_shear, a, b) for a, b in zip(sheared, plain)]
    joint = [swapped(jnp.where(is_low == at_upper, a, b)) for a, b in zip(far, near)]

    stack = lambda tiles: jnp.concatenate(tiles, axis=0)
    ghosts, joint = stack(ghosts), stack(joint)
    strip = []
    for f in range(fields):
        strip.append([])
        for z in range(depth):
            k = f * depth + z
            s = own_part[f][z]
            s = jnp.where(wide < 8, turned(ghosts, -8 * k, 1), s)
            s = jnp.where((wide >= 40) & (wide < 48), turned(joint, 40 - 8 * k, 1), s)
            strip[f].append(s)

    strip = advance(strip, depth)
    back = jnp.where(at_lower, lanes - 36, lanes - 44)
    takes = ((wide == 7) & at_lower) | ((wide < 2) & at_upper)
    for z in range(depth):
        moved = [pltpu.roll(strip[f][z], back, 1) for f in range(8)]
        rho, my = moved[0], moved[2]
        moved[2] = my + (side_f * SHEAR_SPEED) * rho
        moved[4] = moved[4] + (side_f * SHEAR_SPEED) * my + (0.5 * SHEAR_SPEED * SHEAR_SPEED) * rho
        for f in range(8):
            strip[f][z] = jnp.where(takes, moved[f], strip[f][z])
    strip = advance(strip, depth)

    inner = wide[:rows]
    for f in range(8):
        for z in range(depth):
            s = strip[f][z][:rows]
            new = 0.5 * (state_ref[f, z] + jnp.where(inner < 4, turned(s, -8, 1), s))
            keep = (inner >= 4) & (inner < lanes - 8)
            out_ref[f, z] = jnp.where(keep, out_ref[f, z], new)

    at_edges(await_sent_edges)
    sides(lambda copy: copy.wait_send(), False)
    for copy in rims:
        copy.wait_send()


def write_out(new_ref, out_ref, sem):
    copy = pltpu.make_async_copy(new_ref, out_ref, sem)
    copy.start()
    copy.wait()


def on_device(nx, ny, state, offsets):
    fields, depth, rows, lanes = state.shape
    dma = pltpu.SemaphoreType.DMA
    plane = lambda *sizes: pltpu.VMEM((*sizes, lanes), jnp.float32)
    lines = 2 * fields * depth
    new = pl.pallas_call(
        functools.partial(kernel, nx, ny),
        out_shape=pltpu.VMEM(state.shape, state.dtype),
        in_specs=[
            pl.BlockSpec(memory_space=pltpu.SMEM),
            pl.BlockSpec(memory_space=pl.ANY),
        ],
        out_specs=pl.BlockSpec(memory_space=pltpu.VMEM),
        scratch_shapes=[
            plane(fields, depth, rows), plane(2, 8),
            plane(lines), plane(lines + 8), plane(lines + 8), plane(lines + 8),
            plane(2, 8 * ny), plane(2, 3, 8), plane(rows * ny + 8),
            dma, dma((2,)), dma((2, 3)), dma((2, 3)), dma((2,)), dma((2,)),
            dma,
        ],
        compiler_params=pltpu.CompilerParams(
            collective_id=0, has_side_effects=True
        ),
    )(offsets, state)
    return pl.pallas_call(
        write_out,
        out_shape=jax.ShapeDtypeStruct(state.shape, state.dtype),
        in_specs=[pl.BlockSpec(memory_space=pltpu.VMEM)],
        out_specs=pl.BlockSpec(memory_space=pl.ANY),
        scratch_shapes=[dma],
        compiler_params=pltpu.CompilerParams(vmem_limit_bytes=1 << 20),
    )(new)


def solution(mesh):
    nx, ny = mesh.shape["gx"], mesh.shape["gy"]
    return jax.shard_map(
        functools.partial(on_device, nx, ny),
        mesh=mesh,
        in_specs=(P(None, None, "gy", "gx"), P()),
        out_specs=P(None, None, "gy", "gx"),
        check_vma=False,
    )
```
